32 devices in a mesh: dp: 8 (over y, x, core), seq: 4 (over z).
Axes of the slice: x: 2, y: 2, z: 4, core: 2. Of those that a mesh axis runs over, the one named last changes fastest.
Arguments:
- queries: bfloat16 [8192, 8192], P(('dp', 'seq')), may hold values from -60 to 60
- keys: bfloat16 [8192, 1024], P(('dp', 'seq')), may hold values from -60 to 60
- values: bfloat16 [8192, 1024], P(('dp', 'seq')), may hold values from -6 to 6
- plan: int32 [8192], P(('dp', 'seq')), may hold values from 0 to 8191, as said below
- segment_ids: int32 [8192], P(('dp', 'seq')), may hold values from 0 to 63, as said below
Outputs:
- attended: bfloat16 [8192, 8192], P(('dp', 'seq'))
The draws below stay inside these ranges and needn't reach their ends.
Inputs may be any that keep to these rules, and one draw needn't show every extreme that they name: `plan`: A permutation of the owner rows. The rows of one device go exactly 8 to each device (owner rows d * 256 to (d + 1) * 256 - 1 belong to device d), in random order among the device's rows. `segment_ids`: documents are runs of equal ids that never fall; every length is a multiple of 128; no document crosses a boundary of the aligned blocks of 1024 owner rows; one document fills a whole block.
All inputs are finite; a program needn't handle non-finite values.
Results may differ from the reference program's by a relative error of at most 0.0053.
Values may be sent and summed in bfloat16 or wider, within the bound.
A program may use at most 128 MiB of HBM per device.

```python
import jax
import jax.numpy as jnp
from jax import lax

H = 64
KVH = 8
HD = 128
TOK_DEV = 256
TOKENS = 8192
GROUP = 1024


def make_plan(key):
    devices = TOKENS // TOK_DEV
    share = TOK_DEV // devices
    alpha = jax.random.permutation(jax.random.fold_in(key, 101), devices).astype(jnp.int32)
    beta = jax.random.permutation(jax.random.fold_in(key, 102), devices).astype(jnp.int32)
    gamma = jax.random.permutation(jax.random.fold_in(key, 103), devices).astype(jnp.int32)
    slots = jnp.arange(TOK_DEV, dtype=jnp.int32)
    blocks = slots // share
    target = alpha[(beta[:, None] + gamma[blocks][None, :]) % devices]
    owner_rows = target * TOK_DEV + slots[None, :]
    shuffle_keys = jax.random.split(jax.random.fold_in(key, 104), devices)
    shuffles = jax.vmap(lambda single: jax.random.permutation(single, TOK_DEV))(shuffle_keys).astype(jnp.int32)
    placed = jnp.take_along_axis(owner_rows, shuffles, axis=1)
    return placed.reshape(TOKENS).astype(jnp.int32)


def draw_plan(key, part):
    return make_plan(key)


def draw_segment_ids(key, part):
    unit = TOK_DEV // 2
    units = TOKENS // unit
    per_group = GROUP // unit
    groups = units // per_group
    places = jnp.arange(units, dtype=jnp.int32)
    inside = places % per_group
    rolls = jax.random.randint(jax.random.fold_in(key, 201), (units,), 0, 20).astype(jnp.int32)
    limit = jnp.where(inside % 2 == 1, 3, 9)
    cuts = jnp.where(rolls < limit, 1, 0).astype(jnp.int32)
    whole = jax.random.randint(jax.random.fold_in(key, 202), (), 0, groups).astype(jnp.int32)
    cuts = jnp.where(places // per_group == whole, 0, cuts)
    cuts = jnp.where(inside == 0, 1, cuts)
    cuts = jnp.where(places == units - 1, 1, cuts)
    labels = lax.cummax(jnp.where(cuts == 1, places, jnp.zeros_like(places)), axis=0)
    return jnp.repeat(labels, unit).astype(jnp.int32)


def draw_queries(key, part):
    base = jnp.clip(jax.random.normal(jax.random.fold_in(key, 402), (TOKENS, H * HD), jnp.float32), -6.0, 6.0)
    return base.astype(jnp.bfloat16)


def draw_keys(key, part):
    base = jnp.clip(jax.random.normal(jax.random.fold_in(key, 502), (TOKENS, KVH * HD), jnp.float32), -6.0, 6.0)
    return base.astype(jnp.bfloat16)


def block_levels(stream_key, extent, cuts, low, top_value):
    def one(position, parts):
        heights = jax.random.uniform(jax.random.fold_in(jax.random.fold_in(stream_key, 6), position), (parts,), jnp.float32, low / len(cuts), top_value / len(cuts))
        return jnp.repeat(jnp.exp(heights), extent[position] // parts).reshape((-1,) + (1,) * (len(extent) - position - 1))

    loudness = one(*cuts[0])
    for cut in cuts[1:]:
        loudness = loudness * one(*cut)
    return loudness


def scatter_about(stream_key, dims, deviation, most, cuts=(), kind=jnp.bfloat16):
    values = jax.random.normal(stream_key, dims, jnp.float32) * deviation
    if len(cuts) > 0:
        values = block_levels(stream_key, dims, cuts, -0.22, 0.18) * values
    return jnp.clip(values, min=-most, max=most).astype(kind)


def setup_inputs(seed: int = 0) -> dict:
    key_of = jax.random.split(jax.random.key(seed), 6)
    return {
        "queries": draw_queries(jax.random.fold_in(key_of[5], 71), 0),
        "keys": draw_keys(jax.random.fold_in(key_of[5], 71), 0),
        "values": scatter_about(key_of[2], (TOKENS, KVH * HD), 1.0, 6.0, ((0, 32),)),
        "plan": draw_plan(jax.random.fold_in(key_of[5], 71), 0),
        "segment_ids": draw_segment_ids(jax.random.fold_in(key_of[5], 71), 0),
    }


theta_base = 500000.0
tile_rows = 512


def doc_positions(segment_ids):
    places = jnp.arange(segment_ids.shape[0], dtype=jnp.int32)
    starts = jnp.concatenate([jnp.ones((1,), jnp.bool_), segment_ids[1:] != segment_ids[:-1]])
    first = lax.cummax(jnp.where(starts, places, jnp.zeros_like(places)), axis=0)
    return places - first


def rotate(source, positions):
    width = source.shape[-1]
    half = width // 2
    freqs = theta_base ** (-2.0 * jnp.arange(half, dtype=jnp.float32) / width)
    angles = positions.astype(jnp.float32)[:, None] * freqs[None, :]
    cosine = jnp.cos(angles)[:, None, :]
    sine = jnp.sin(angles)[:, None, :]
    floats = source.astype(jnp.float32)
    lower = floats[..., :half]
    upper = floats[..., half:]
    turned = jnp.concatenate([lower * cosine - upper * sine, upper * cosine + lower * sine], axis=-1)
    return turned.astype(jnp.bfloat16)


def masked_block(query_block, key_part, value_part, query_ids, key_ids, anchor):
    count = query_block.shape[0]
    reach = key_part.shape[0]
    scores = jnp.einsum("qkgd,tkd->kgqt", query_block.astype(jnp.float32), key_part.astype(jnp.float32)) * (HD ** -0.5)
    query_rows = anchor + jnp.arange(count, dtype=jnp.int32)
    key_rows = jnp.arange(reach, dtype=jnp.int32)
    allowed = (key_rows[None, :] <= query_rows[:, None]) & (key_ids[None, :] == query_ids[:, None])
    scores = jnp.where(allowed, scores, -jnp.inf)
    peak = jnp.max(scores, axis=-1, keepdims=True)
    weights = jnp.exp(scores - peak)
    totals = jnp.sum(weights, axis=-1)
    rounded = lax.optimization_barrier(weights.astype(jnp.bfloat16)).astype(jnp.float32)
    mixed = jnp.einsum("kgqt,tkd->kgqd", rounded, value_part.astype(jnp.float32))
    result = mixed / totals[..., None]
    return jnp.transpose(result, (2, 0, 1, 3)).astype(jnp.bfloat16)


def reference(queries, keys, values, plan, segment_ids):
    total = queries.shape[0]
    per_kv = H // KVH
    own_q = jnp.zeros_like(queries).at[plan].set(queries)
    own_k = jnp.zeros_like(keys).at[plan].set(keys)
    own_v = jnp.zeros_like(values).at[plan].set(values)
    positions = doc_positions(segment_ids)
    rot_q = rotate(own_q.reshape(total, H, HD), positions).reshape(total, KVH, per_kv, HD)
    rot_k = rotate(own_k.reshape(total, KVH, HD), positions)
    own_v = own_v.reshape(total, KVH, HD)

    def one_group(number):
        start = number * GROUP
        group_q = lax.dynamic_slice_in_dim(rot_q, start, GROUP, 0)
        group_k = lax.dynamic_slice_in_dim(rot_k, start, GROUP, 0)
        group_v = lax.dynamic_slice_in_dim(own_v, start, GROUP, 0)
        group_ids = lax.dynamic_slice_in_dim(segment_ids, start, GROUP, 0)
        pieces = []
        for block in range(GROUP // tile_rows):
            low = block * tile_rows
            high = low + tile_rows
            pieces.append(masked_block(group_q[low:high], group_k[:high], group_v[:high], group_ids[low:high], group_ids[:high], low))
        return jnp.concatenate(pieces, axis=0)

    outputs = lax.map(one_group, jnp.arange(total // GROUP, dtype=jnp.int32))
    own_out = outputs.reshape(total, H * HD)
    return own_out[plan]
```

```python
import functools

import jax
import jax.numpy as jnp
import numpy as np
from jax import lax
from jax.experimental import pallas as pl
from jax.experimental.pallas import tpu as pltpu
from jax.sharding import PartitionSpec as P

H = 64
KVH = 8
HD = 128
theta_base = 500000.0
UNIT = 128
LANES = 128
LOG2E = 1.4426950408889634
MESH = pl.DeviceIdType.MESH
CROSS = (((1,), (1,)), ((), ()))


def dot(a, b):
    return jnp.dot(a, b, preferred_element_type=jnp.float32)


def dot_t(a, b):
    return lax.dot_general(a, b, CROSS, preferred_element_type=jnp.float32)


def turn(x, c, s):
    return (x * c + pltpu.roll(x, HD // 2, 1) * s).astype(jnp.bfloat16)


def flip(d, w):
    return d + w * (1 - 2 * ((d // w) % 2))


def frequencies():
    exponents = np.arange(HD // 2, dtype=np.float32)
    return np.float32(theta_base) ** (np.float32(-2.0) * exponents / np.float32(HD))


def shared_bits(dps):
    return [w for w in (2, 4) if 2 * w <= dps]


def travel(
    seqs, dps, q, k, v, plan, seg, out,
    plan_v, seg_v, kraw, vraw, qs, kvs, qr, kvz, ob, home, ks, vs,
    onehot, onehot_t, sort, unsort, sort_half, unsort_half, bias, firsts, part_q,
    stiles, sgot, zspots, idz, idg,
    small_sem, kv_load, q_load,
    v_send, v_recv, v_own, k_send, k_recv, k_own,
    q_send, q_recv, q_own, o_send, o_recv, o_own,
    s_send, s_recv, iz_send, iz_recv, i_send, i_recv, zs_send, zs_recv, z_send, z_recv,
):
    rows = q.shape[0]
    per_kv = H // KVH
    wide = per_kv * HD
    chunk = rows // seqs
    share = chunk // dps
    slab = rows // dps
    group = rows * seqs
    upd = rows // UNIT
    hr = rows // 2
    bits = shared_bits(dps)
    nsh = len(bits)
    plain = KVH - nsh
    items = KVH + nsh
    half = dps // 2
    early = 4
    me = lax.axis_index("dp")
    z = lax.axis_index("seq")
    f32, bf16 = jnp.float32, jnp.bfloat16

    def remote(src, dst, send, recv, where):
        return pltpu.make_async_remote_copy(
            src_ref=src, dst_ref=dst, send_sem=send, recv_sem=recv,
            device_id=where, device_id_type=MESH,
        )

    def slab_of(d):
        return pl.ds(pl.multiple_of(d * slab, slab), slab)

    def cols(h, width):
        return pl.ds(pl.multiple_of(h * width, width), width)

    peers = [lax.rem(me + n, dps) for n in range(1, dps)]
    planes = [lax.rem(z + n, seqs) for n in range(1, seqs)]

    def rank_of(d, w):
        return (d // (2 * w)) * w + d % w

    def side(w):
        bit = (me // w) % 2
        inner = rank_of(me, w)
        found = []
        for n in range(1, half):
            c = lax.rem(inner + n, half)
            found.append((c // w) * (2 * w) + bit * w + c % w)
        return found

    smalls = [
        pltpu.make_async_copy(plan, plan_v, small_sem.at[0]),
        pltpu.make_async_copy(seg, seg_v, small_sem.at[1]),
    ]
    for copy in smalls:
        copy.start()
    v_load = pltpu.make_async_copy(v, vraw, kv_load.at[0])
    k_load = pltpu.make_async_copy(k, kraw, kv_load.at[1])
    v_load.start()
    k_load.start()

    barrier = pltpu.get_barrier_semaphore()

    for d in peers:
        pl.semaphore_signal(barrier, inc=1, device_id=(d, z), device_id_type=MESH)
    for p in planes:
        pl.semaphore_signal(barrier, inc=1, device_id=(me, p), device_id_type=MESH)

    def q_in(h):
        return pltpu.make_async_copy(q.at[:, cols(h, wide)], qs.at[h], q_load.at[h])

    @pl.loop(0, KVH)
    def _(h):
        q_in(h).start()

    lane = lax.broadcasted_iota(jnp.int32, (1, LANES), 1)
    smalls[1].wait()
    marks = jnp.zeros((1, LANES), f32)
    for u in range(upd):
        mine = seg_v[0:1, u * UNIT : u * UNIT + 1].astype(f32)
        marks = jnp.where(lane == z * upd + u, mine, marks)
    idz[z] = jnp.broadcast_to(marks, (8, LANES))

    row = lax.broadcasted_iota(jnp.int32, (rows, rows), 0)
    col = lax.broadcasted_iota(jnp.int32, (rows, rows), 1)
    eye = jnp.where(row == col, 1.0, 0.0).astype(bf16)
    smalls[0].wait()
    target = (plan_v[...] // rows).astype(f32)
    spread = jnp.broadcast_to(target, (16, rows)).astype(bf16)
    upright = dot_t(eye, spread)[:, 0:1]
    ahead = jnp.where((upright == target) & (row < col), 1.0, 0.0)
    slot = target * share + jnp.sum(ahead, axis=0, keepdims=True)
    place = jnp.where(slot == row.astype(f32), 1.0, 0.0).astype(bf16)
    onehot[...] = place
    onehot_t[...] = dot_t(eye, place).astype(bf16)

    spot = plan_v[...] % group
    high = jnp.broadcast_to((spot // 32).astype(f32), (8, rows))
    low = jnp.broadcast_to((spot % 32).astype(f32), (8, rows))
    lines = jnp.concatenate([high, low], axis=0).astype(bf16)
    flat = dot_t(lines, place)
    flat = flat[0:8] * 32.0 + flat[8:16]
    upright = dot_t(place, lines)
    spot_up = upright[:, 0:1] * 32.0 + upright[:, 8:9]
    sub = lax.broadcasted_iota(jnp.int32, (8, LANES), 0)
    shifted = [pltpu.roll(flat, (rows - d * slab) % rows, 1)[:, :LANES] for d in range(dps)]
    for d in range(dps):
        tile = shifted[d]
        for n, w in enumerate(bits):
            tile = jnp.where(sub == n + 1, shifted[flip(d, w)], tile)
        stiles[d] = tile
    sgot[me] = stiles[me]

    pl.semaphore_wait(barrier, dps + seqs - 2)

    def id_hop(n, p, origin):
        block = idz.at[origin]
        return remote(block, block, iz_send.at[n - 1], iz_recv.at[origin], (me, p))

    for n, p in enumerate(planes, 1):
        id_hop(n, p, z).start()

    for d in peers:
        remote(stiles.at[d], sgot.at[me], s_send, s_recv, (d, z)).start()

    most = pl.ds(0, rows - slab)
    lower, upper = pl.ds(0, HD), pl.ds(HD, HD)

    def kv_push(h, item, w, part, send, recv, own):
        for d in peers:
            origin = d if w == 0 else flip(d, w)
            remote(
                kvs.at[h, slab_of(origin), part], kvz.at[z, item, slab_of(me), part],
                send.at[item], recv.at[item], (d, z),
            ).start()
        kv_local(h, item, w, part, own).start()

    def kv_local(h, item, w, part, own):
        origin = me if w == 0 else flip(me, w)
        return pltpu.make_async_copy(
            kvs.at[h, slab_of(origin), part], kvz.at[z, item, slab_of(me), part], own.at[item]
        )

    def kv_all(item, part, send, recv):
        block = kvz.at[z, item, most, part]
        return remote(block, block, send.at[item], recv.at[item], (me, z))

    def kv_own(item, part, own):
        block = kvz.at[z, item, slab_of(me), part]
        return pltpu.make_async_copy(block, block, own.at[item])

    v_load.wait()

    def v_pair(pair):
        both = dot(onehot[...], vraw[:, cols(pair, 2 * HD)]).astype(bf16)
        for n in range(2):
            h = pair * 2 + n
            kvs[h, :, HD:] = both[:, n * HD : (n + 1) * HD]
            kv_push(h, h, 0, upper, v_send, v_recv, v_own)

    pl.loop(0, early // 2)(v_pair)

    for n, p in enumerate(planes, 1):
        id_hop(n, p, p).wait_recv()
    idg[me] = functools.reduce(jnp.add, [idz[p] for p in range(seqs)])
    for d in peers:
        remote(idg.at[me], idg.at[me], i_send, i_recv, (d, z)).start()

    pl.loop(early // 2, KVH // 2)(v_pair)

    for n, w in enumerate(bits):
        kv_push(plain + n, KVH + n, w, upper, v_send, v_recv, v_own)

    def hop(up, t, origin, item, part=None):
        step = 1 if up else -1
        block = kvz.at[origin, item] if part is None else kvz.at[origin, item, :, part]
        return remote(
            block, block,
            z_send.at[(0 if up else 1) * seqs + t, item], z_recv.at[origin, item], (me, z + step),
        )

    def leave(item, part):
        @pl.when(z + 1 < seqs)
        def _():
            hop(True, 0, z, item, part).start()

        @pl.when(z > 0)
        def _():
            hop(False, 0, z, item, part).start()

    def v_leave(item):
        kv_all(item, upper, v_send, v_recv).wait_recv()
        kv_own(item, upper, v_own).wait()
        leave(item, upper)

    pl.loop(0, early)(v_leave)

    def ids_all():
        some = idg.at[pl.ds(0, dps - 1)]
        return remote(some, some, i_send, i_recv, (me, z))

    ids_all().wait_recv()
    ids = jnp.concatenate([idg[d, 0:1, :] for d in range(dps)], axis=0)
    first = jnp.full((dps, LANES), float(group), f32)
    for u in range(seqs * upd):
        same = ids == ids[:, u : u + 1]
        first = jnp.where(same, jnp.minimum(first, float(u * UNIT)), first)
    firsts[...] = first

    def starts(spots, table):
        unit = jnp.floor(spots * (1.0 / UNIT))
        hit = lane.astype(f32) == unit
        return jnp.sum(jnp.where(hit, table, 0.0), axis=1, keepdims=True)

    freqs = jnp.zeros((1, HD), f32)
    for j, freq in enumerate(frequencies()):
        freqs = jnp.where(lane % (HD // 2) == j, freq, freqs)
    table = jnp.concatenate(
        [jnp.broadcast_to(first[d : d + 1], (slab, LANES)) for d in range(dps)], axis=0
    )
    angles = (spot_up - starts(spot_up, table)) * freqs
    cosine = jnp.cos(angles)
    sine = jnp.sin(angles) * jnp.where(lane < HD // 2, -1.0, 1.0)

    k_load.wait()

    @pl.loop(0, KVH // 2)
    def _(pair):
        both = dot(onehot[...], kraw[:, cols(pair, 2 * HD)])
        for n in range(2):
            h = pair * 2 + n
            kvs[h, :, :HD] = turn(both[:, n * HD : (n + 1) * HD], cosine, sine)
            kv_push(h, h, 0, lower, k_send, k_recv, k_own)

    for n, w in enumerate(bits):
        kv_push(plain + n, KVH + n, w, lower, k_send, k_recv, k_own)

    def spots_all():
        some = sgot.at[pl.ds(0, dps - 1)]
        return remote(some, some, s_send, s_recv, (me, z))

    spots_all().wait_recv()
    strips = []
    for start in range(0, rows, LANES):
        strip = jnp.zeros((8, LANES), f32)
        for d in range(start // slab, (start + LANES) // slab):
            off = d * slab - start
            inside = (lane >= off) & (lane < off + slab)
            strip = jnp.where(inside, pltpu.roll(sgot[d], off, 1) if off else sgot[d], strip)
        strips.append(strip)
    zspots[z] = jnp.concatenate(strips, axis=1)

    def spots_hop(n, p, origin):
        block = zspots.at[origin]
        return remote(block, block, zs_send.at[n - 1], zs_recv.at[origin], (me, p))

    for n, p in enumerate(planes, 1):
        spots_hop(n, p, z).start()

    pl.loop(early, items)(v_leave)

    def q_turn(h):
        q_in(h).wait()
        x = dot(onehot[...], qs[h])
        for g in range(per_kv):
            qs[h, :, g * HD : (g + 1) * HD] = turn(x[:, g * HD : (g + 1) * HD], cosine, sine)

    def q_plain(h):
        q_turn(h)
        for d in peers:
            remote(
                qs.at[h, slab_of(d)], qr.at[h, slab_of(me)],
                q_send.at[h], q_recv.at[h], (d, z),
            ).start()
        pltpu.make_async_copy(
            qs.at[h, slab_of(me)], qr.at[h, slab_of(me)], q_own.at[h]
        ).start()

    def spot_in(sel, rank):
        return pl.ds(pl.multiple_of(sel * hr + rank * slab, slab), slab)

    def q_shared(h, w):
        q_turn(h)
        for sel in range(2):
            for d in side(w):
                remote(
                    qs.at[h, slab_of(flip(d, w) if sel else d)], qr.at[h, spot_in(sel, rank_of(me, w))],
                    q_send.at[h], q_recv.at[h], (d, z),
                ).start()
            pltpu.make_async_copy(
                qs.at[h, slab_of(flip(me, w) if sel else me)], qr.at[h, spot_in(sel, rank_of(me, w))],
                q_own.at[h],
            ).start()

    def o_plain(h):
        for d in peers:
            remote(
                ob.at[h, slab_of(d)], home.at[h, slab_of(me)],
                o_send.at[h], o_recv.at[h], (d, z),
            ).start()
        pltpu.make_async_copy(
            ob.at[h, slab_of(me)], home.at[h, slab_of(me)], o_own.at[h]
        ).start()

    def o_shared(h, item, w, sel):
        target = slab_of(flip(me, w) if sel else me)
        for d in side(w):
            remote(
                ob.at[h, spot_in(sel, rank_of(d, w))], home.at[h, target],
                o_send.at[item], o_recv.at[item], (d, z),
            ).start()
        pltpu.make_async_copy(
            ob.at[h, spot_in(sel, rank_of(me, w))], home.at[h, target], o_own.at[item]
        ).start()

    def away(buf, h, index, send, recv, count):
        block = buf.at[h, pl.ds(0, count)]
        return remote(block, block, send.at[index], recv.at[index], (me, z))

    def stay(buf, h, index, own, count):
        block = buf.at[h, pl.ds(0, count)]
        return pltpu.make_async_copy(block, block, own.at[index])

    def arrival(s):
        inner = s % chunk
        return (inner // share) * (seqs * share) + (s // chunk) * share + inner % share

    def arrival_half(s):
        inner = s % (chunk // 2)
        return (inner // share) * slab + (s // (chunk // 2)) * share + inner % share

    def source_half(s, w):
        inner = s % (chunk // 2)
        rank = inner // share
        d = (rank // w) * (2 * w) + ((me // w) % 2) * w + rank % w
        return d * slab + (s // (chunk // 2)) * share + inner % share

    def orders():
        sort[...] = jnp.where(col == arrival(row), 1.0, 0.0).astype(bf16)
        unsort[...] = jnp.where(row == arrival(col), 1.0, 0.0).astype(bf16)
        row_half, col_half = row[:hr, :hr], col[:hr, :hr]
        sort_half[...] = jnp.where(col_half == arrival_half(row_half), 1.0, 0.0).astype(bf16)
        unsort_half[...] = jnp.where(row_half == arrival_half(col_half), 1.0, 0.0).astype(bf16)

    def halves(x):
        top = jnp.floor(x * (1.0 / 32.0))
        return jnp.concatenate([top, x - 32.0 * top], axis=0).astype(bf16)

    def prepare():
        for n, p in enumerate(planes, 1):
            spots_hop(n, p, p).wait_recv()
        planed = []
        for p in range(seqs):
            s = dot_t(halves(zspots[p]), sort[...])
            planed.append(s[0:8] * 32.0 + s[8:16])
        keyed = []
        for start in range(0, group, LANES):
            strip = jnp.zeros((8, LANES), f32)
            for piece in range(start // chunk, (start + LANES) // chunk):
                c, p = piece // seqs, piece % seqs
                source = c * chunk
                base = source // LANES * LANES
                off = piece * chunk - start
                moved = planed[p][:, base : base + LANES]
                shift = (off - (source - base)) % LANES
                if shift:
                    moved = pltpu.roll(moved, shift, 1)
                strip = jnp.where((lane >= off) & (lane < off + chunk), moved, strip)
            keyed.append(strip)
        key = jnp.concatenate(keyed, axis=1)

        def fence(order, low_row, count, spots, key_row, owner):
            begin = starts(spots, firsts[pl.ds(owner, 1), :])
            keep = (key[key_row : key_row + 1] <= spots) & (key[key_row : key_row + 1] >= begin)
            bias[order, low_row : low_row + count] = jnp.where(keep, 0.0, -1e30)

        here = halves(zspots[z])
        up = dot_t(sort[...], here)
        fence(0, 0, rows, up[:, 0:1] * 32.0 + up[:, 8:9], 0, me)
        for n, w in enumerate(bits):
            pick = jnp.where(col[:hr] == source_half(row[:hr], w), 1.0, 0.0).astype(bf16)
            up = dot_t(pick, here)
            fence(n + 1, 0, hr, up[:, 0:1] * 32.0 + up[:, 8:9], 0, me)
            m = n + 1
            spots = up[:, m : m + 1] * 32.0 + up[:, m + 8 : m + 9]
            fence(n + 1, hr, hr, spots, m, flip(me, w))

    def attend(h, item, order, base, count, forth, back):
        here = pl.ds(base, count)
        x = dot(forth[...], qr[h, here]).astype(bf16)
        piece = count // seqs
        for p in range(seqs):
            both = dot(sort[...], kvz[p, item]).astype(bf16)
            for c in range(seqs):
                spot_rows = slice(c * rows + p * chunk, c * rows + (p + 1) * chunk)
                ks[spot_rows] = both[c * chunk : (c + 1) * chunk, :HD]
                vs[spot_rows] = both[c * chunk : (c + 1) * chunk, HD:]
        for c in range(seqs):
            reach = (c + 1) * rows
            inner = slice(c * piece, (c + 1) * piece)
            block = jnp.concatenate(
                [x[inner, g * HD : (g + 1) * HD] for g in range(per_kv)], axis=0
            )
            s = dot_t(block, ks[:reach])
            s = s.reshape(per_kv, piece, reach) * (HD ** -0.5 * LOG2E)
            s = s + bias[order, pl.ds(base + c * piece, piece), :reach][None]
            e = jnp.exp2(s - jnp.max(s, axis=-1, keepdims=True))
            total = jnp.sum(e, axis=-1, keepdims=True).reshape(per_kv * piece, 1)
            mixed = dot(e.astype(bf16).reshape(per_kv * piece, reach), vs[:reach])
            mixed = (mixed / total).astype(bf16)
            for g in range(per_kv):
                part_q[inner, g * HD : (g + 1) * HD] = mixed[g * piece : (g + 1) * piece]
        ob[h, here] = dot(back[...], part_q[:count]).astype(bf16)

    def finish(h):
        away(home, h, h, o_send, o_recv, rows - slab).wait_recv()
        stay(home, h, h, o_own, slab).wait()
        out[:, cols(h, wide)] = dot(onehot_t[...], home[h]).astype(bf16)

    def finish_shared(h, n):
        for item in (h, KVH + n):
            away(home, h, item, o_send, o_recv, hr - slab).wait_recv()
            stay(home, h, item, o_own, slab).wait()
        out[:, cols(h, wide)] = dot(onehot_t[...], home[h]).astype(bf16)

    done = plain // 2

    @pl.loop(0, items + seqs - 1)
    def _(i):
        @pl.when(i < items)
        def _():
            kv_all(i, lower, k_send, k_recv).wait_recv()
            kv_own(i, lower, k_own).wait()
            leave(i, lower)

        for t in range(1, seqs):
            live = (i >= t) & (i - t < items)

            @pl.when(live & (z >= t))
            def _():
                hop(True, t, z - t, i - t).wait_recv()

                @pl.when(z + 1 < seqs)
                def _():
                    hop(True, t, z - t, i - t).start()

            @pl.when(live & (z + t < seqs))
            def _():
                hop(False, t, z + t, i - t).wait_recv()

                @pl.when(z > 0)
                def _():
                    hop(False, t, z + t, i - t).start()

        @pl.when(i < plain // 2)
        def _():
            q_plain(2 * i)
            q_plain(2 * i + 1)

        @pl.when(i == plain // 2)
        def _():
            for h in range(plain // 2 * 2, plain):
                q_plain(h)
            for n, w in enumerate(bits):
                q_shared(plain + n, w)

        @pl.when(i == min(2, seqs - 1))
        def _():
            orders()
            prepare()

        j = i - (seqs - 1)

        @pl.when((j >= 0) & (j < plain))
        def _():
            away(qr, j, j, q_send, q_recv, rows - slab).wait_recv()
            stay(qr, j, j, q_own, slab).wait()
            attend(j, j, 0, 0, rows, sort, unsort)
            o_plain(j)

        if nsh:
            @pl.when((j >= plain) & (j < KVH))
            def _():
                away(qr, j, j, q_send, q_recv, rows - 2 * slab).wait_recv()
                stay(qr, j, j, q_own, 2 * slab).wait()

            @pl.when(j >= plain)
            def _():
                n = (j - plain) % nsh
                sel = (j - plain) // nsh
                base = pl.multiple_of(sel * hr, hr)
                attend(plain + n, j, n + 1, base, hr, sort_half, unsort_half)

            for sel in range(2):
                for n, w in enumerate(bits):
                    @pl.when(j == plain + sel * nsh + n)
                    def _():
                        o_shared(plain + n, plain + sel * nsh + n, w, sel)

        @pl.when(i == items + seqs - 3)
        def _():
            pl.loop(0, done)(finish)

    pl.loop(done, plain)(finish)
    for n in range(nsh):
        finish_shared(plain + n, n)

    ids_all().wait_send()
    spots_all().wait_send()
    for n, p in enumerate(planes, 1):
        id_hop(n, p, z).wait_send()
        spots_hop(n, p, z).wait_send()

    @pl.loop(0, items)
    def _(item):
        kv_all(item, upper, v_send, v_recv).wait_send()
        kv_all(item, lower, k_send, k_recv).wait_send()
        for t in range(seqs - 1):

            @pl.when((z >= t) & (z + 1 < seqs))
            def _():
                hop(True, t, z - t, item).wait_send()

            @pl.when((z + t < seqs) & (z > 0))
            def _():
                hop(False, t, z + t, item).wait_send()

    @pl.loop(0, plain)
    def _(h):
        away(qr, h, h, q_send, q_recv, rows - slab).wait_send()
        away(ob, h, h, o_send, o_recv, rows - slab).wait_send()

    for n in range(nsh):
        h = plain + n
        away(qr, h, h, q_send, q_recv, rows - 2 * slab).wait_send()
        for item in (h, KVH + n):
            away(ob, h, item, o_send, o_recv, hr - slab).wait_send()


def per_device(queries, keys, values, plan, segment_ids):
    rows = queries.shape[0]
    seqs = lax.axis_size("seq")
    dps = lax.axis_size("dp")
    group = rows * seqs
    per_kv = H // KVH
    wide = per_kv * HD
    nsh = len(shared_bits(dps))
    items = KVH + nsh
    anywhere = pl.BlockSpec(memory_space=pltpu.HBM)
    dma = pltpu.SemaphoreType.DMA
    bf16, f32, i32 = jnp.bfloat16, jnp.float32, jnp.int32
    return pl.pallas_call(
        functools.partial(travel, seqs, dps),
        in_specs=[anywhere] * 5,
        out_specs=pl.BlockSpec(memory_space=pltpu.VMEM),
        out_shape=pltpu.VMEM(queries.shape, bf16),
        scratch_shapes=[
            pltpu.VMEM((1, rows), i32),
            pltpu.VMEM((1, rows), i32),
            pltpu.VMEM((rows, KVH * HD), bf16),
            pltpu.VMEM((rows, KVH * HD), bf16),
            pltpu.VMEM((KVH, rows, wide), bf16),
            pltpu.VMEM((KVH, rows, 2 * HD), bf16),
            pltpu.VMEM((KVH, rows, wide), bf16),
            pltpu.VMEM((seqs, items, rows, 2 * HD), bf16),
            pltpu.VMEM((KVH, rows, wide), bf16),
            pltpu.VMEM((KVH, rows, wide), bf16),
            pltpu.VMEM((group, HD), bf16),
            pltpu.VMEM((group, HD), bf16),
            pltpu.VMEM((rows, rows), bf16),
            pltpu.VMEM((rows, rows), bf16),
            pltpu.VMEM((rows, rows), bf16),
            pltpu.VMEM((rows, rows), bf16),
            pltpu.VMEM((rows // 2, rows // 2), bf16),
            pltpu.VMEM((rows // 2, rows // 2), bf16),
            pltpu.VMEM((1 + nsh, rows, group), f32),
            pltpu.VMEM((dps, LANES), f32),
            pltpu.VMEM((rows, wide), bf16),
            pltpu.VMEM((dps, 8, LANES), f32),
            pltpu.VMEM((dps, 8, LANES), f32),
            pltpu.VMEM((seqs, 8, rows), f32),
            pltpu.VMEM((seqs, 8, LANES), f32),
            pltpu.VMEM((dps, 8, LANES), f32),
            dma((2,)), dma((2,)), dma((KVH,)),
            dma((items,)), dma((items,)), dma((items,)),
            dma((items,)), dma((items,)), dma((items,)),
            dma((KVH,)), dma((KVH,)), dma((KVH,)),
            dma((items,)), dma((items,)), dma((items,)),
            dma, dma, dma((seqs,)), dma((seqs,)), dma, dma, dma((seqs,)), dma((seqs,)),
            dma((2 * seqs, items)), dma((seqs, items)),
        ],
        compiler_params=pltpu.CompilerParams(
            collective_id=0, has_side_effects=True, vmem_limit_bytes=56 * 1024 * 1024
        ),
    )(queries, keys, values, plan[None, :], segment_ids[None, :])


def solution(mesh):
    return jax.shard_map(
        per_device,
        mesh=mesh,
        in_specs=(
            P(("dp", "seq"), None),
            P(("dp", "seq"), None),
            P(("dp", "seq"), None),
            P(("dp", "seq")),
            P(("dp", "seq")),
        ),
        out_specs=P(("dp", "seq"), None),
        check_vma=False,
    )
```

```python
import functools

import jax
import jax.numpy as jnp
import numpy as np
from jax import lax
from jax.experimental import pallas as pl
from jax.experimental.pallas import tpu as pltpu
from jax.sharding import PartitionSpec as P

H = 64
KVH = 8
HD = 128
theta_base = 500000.0
UNIT = 128
LANES = 128
LOG2E = 1.4426950408889634
MESH = pl.DeviceIdType.MESH
CROSS = (((1,), (1,)), ((), ()))


def dot(a, b):
    return jnp.dot(a, b, preferred_element_type=jnp.float32)


def dot_t(a, b):
    return lax.dot_general(a, b, CROSS, preferred_element_type=jnp.float32)


def turn(x, c, s):
    return (x * c + pltpu.roll(x, HD // 2, 1) * s).astype(jnp.bfloat16)


def flip(d, w):
    return d + w * (1 - 2 * ((d // w) % 2))


def frequencies():
    exponents = np.arange(HD // 2, dtype=np.float32)
    return np.float32(theta_base) ** (np.float32(-2.0) * exponents / np.float32(HD))


def shared_bits(dps):
    return [w for w in (2, 4) if 2 * w <= dps]


def travel(
    seqs, dps, q, k, v, plan, seg, out,
    plan_v, seg_v, kraw, vraw, qs, kvs, qr, kvz, ob, home, ks, vs,
    onehot, onehot_t, sort, unsort, sort_half, unsort_half, bias, firsts, part_q,
    stiles, sgot, zspots, idz, idg,
    small_sem, kv_load, q_load,
    v_send, v_recv, v_own, k_send, k_recv, k_own,
    q_send, q_recv, q_own, o_send, o_recv, o_own,
    s_send, s_recv, iz_send, iz_recv, i_send, i_recv, zs_send, zs_recv, z_send, z_recv,
):
    rows = q.shape[0]
    per_kv = H // KVH
    wide = per_kv * HD
    chunk = rows // seqs
    share = chunk // dps
    slab = rows // dps
    group = rows * seqs
    upd = rows // UNIT
    hr = rows // 2
    bits = shared_bits(dps)
    nsh = len(bits)
    plain = KVH - nsh
    items = KVH + nsh
    half = dps // 2
    early = 4
    me = lax.axis_index("dp")
    z = lax.axis_index("seq")
    f32, bf16 = jnp.float32, jnp.bfloat16

    def remote(src, dst, send, recv, where):
        return pltpu.make_async_remote_copy(
            src_ref=src, dst_ref=dst, send_sem=send, recv_sem=recv,
            device_id=where, device_id_type=MESH,
        )

    def slab_of(d):
        return pl.ds(pl.multiple_of(d * slab, slab), slab)

    def cols(h, width):
        return pl.ds(pl.multiple_of(h * width, width), width)

    peers = [lax.rem(me + n, dps) for n in range(1, dps)]
    planes = [lax.rem(z + n, seqs) for n in range(1, seqs)]

    def rank_of(d, w):
        return (d // (2 * w)) * w + d % w

    def side(w):
        bit = (me // w) % 2
        inner = rank_of(me, w)
        found = []
        for n in range(1, half):
            c = lax.rem(inner + n, half)
            found.append((c // w) * (2 * w) + bit * w + c % w)
        return found

    smalls = [
        pltpu.make_async_copy(plan, plan_v, small_sem.at[0]),
        pltpu.make_async_copy(seg, seg_v, small_sem.at[1]),
    ]
    for copy in smalls:
        copy.start()
    v_load = pltpu.make_async_copy(v, vraw, kv_load.at[0])
    k_load = pltpu.make_async_copy(k, kraw, kv_load.at[1])
    v_load.start()
    k_load.start()

    barrier = pltpu.get_barrier_semaphore()

    for d in peers:
        pl.semaphore_signal(barrier, inc=1, device_id=(d, z), device_id_type=MESH)
    for p in planes:
        pl.semaphore_signal(barrier, inc=1, device_id=(me, p), device_id_type=MESH)

    def q_in(h):
        return pltpu.make_async_copy(q.at[:, cols(h, wide)], qs.at[h], q_load.at[h])

    @pl.loop(0, KVH)
    def _(h):
        q_in(h).start()

    lane = lax.broadcasted_iota(jnp.int32, (1, LANES), 1)
    smalls[1].wait()
    marks = jnp.zeros((1, LANES), f32)
    for u in range(upd):
        mine = seg_v[0:1, u * UNIT : u * UNIT + 1].astype(f32)
        marks = jnp.where(lane == z * upd + u, mine, marks)
    idz[z] = jnp.broadcast_to(marks, (8, LANES))

    row = lax.broadcasted_iota(jnp.int32, (rows, rows), 0)
    col = lax.broadcasted_iota(jnp.int32, (rows, rows), 1)
    eye = jnp.where(row == col, 1.0, 0.0).astype(bf16)
    smalls[0].wait()
    target = (plan_v[...] // rows).astype(f32)
    spread = jnp.broadcast_to(target, (16, rows)).astype(bf16)
    upright = dot_t(eye, spread)[:, 0:1]
    ahead = jnp.where((upright == target) & (row < col), 1.0, 0.0)
    slot = target * share + jnp.sum(ahead, axis=0, keepdims=True)
    place = jnp.where(slot == row.astype(f32), 1.0, 0.0).astype(bf16)
    onehot[...] = place
    onehot_t[...] = dot_t(eye, place).astype(bf16)

    spot = plan_v[...] % group
    high = jnp.broadcast_to((spot // 32).astype(f32), (8, rows))
    low = jnp.broadcast_to((spot % 32).astype(f32), (8, rows))
    lines = jnp.concatenate([high, low], axis=0).astype(bf16)
    flat = dot_t(lines, place)
    flat = flat[0:8] * 32.0 + flat[8:16]
    upright = dot_t(place, lines)
    spot_up = upright[:, 0:1] * 32.0 + upright[:, 8:9]
    sub = lax.broadcasted_iota(jnp.int32, (8, LANES), 0)
    shifted = [pltpu.roll(flat, (rows - d * slab) % rows, 1)[:, :LANES] for d in range(dps)]
    for d in range(dps):
        tile = shifted[d]
        for n, w in enumerate(bits):
            tile = jnp.where(sub == n + 1, shifted[flip(d, w)], tile)
        stiles[d] = tile
    sgot[me] = stiles[me]

    pl.semaphore_wait(barrier, dps + seqs - 2)

    def id_hop(n, p, origin):
        block = idz.at[origin]
        return remote(block, block, iz_send.at[n - 1], iz_recv.at[origin], (me, p))

    for n, p in enumerate(planes, 1):
        id_hop(n, p, z).start()

    for d in peers:
        remote(stiles.at[d], sgot.at[me], s_send, s_recv, (d, z)).start()

    most = pl.ds(0, rows - slab)
    lower, upper = pl.ds(0, HD), pl.ds(HD, HD)

    def kv_push(h, item, w, part, send, recv, own):
        for d in peers:
            origin = d if w == 0 else flip(d, w)
            remote(
                kvs.at[h, slab_of(origin), part], kvz.at[z, item, slab_of(me), part],
                send.at[item], recv.at[item], (d, z),
            ).start()
        kv_local(h, item, w, part, own).start()

    def kv_local(h, item, w, part, own):
        origin = me if w == 0 else flip(me, w)
        return pltpu.make_async_copy(
            kvs.at[h, slab_of(origin), part], kvz.at[z, item, slab_of(me), part], own.at[item]
        )

    def kv_all(item, part, send, recv):
        block = kvz.at[z, item, most, part]
        return remote(block, block, send.at[item], recv.at[item], (me, z))

    def kv_own(item, part, own):
        block = kvz.at[z, item, slab_of(me), part]
        return pltpu.make_async_copy(block, block, own.at[item])

    v_load.wait()

    def v_pair(pair):
        both = dot(onehot[...], vraw[:, cols(pair, 2 * HD)]).astype(bf16)
        for n in range(2):
            h = pair * 2 + n
            kvs[h, :, HD:] = both[:, n * HD : (n + 1) * HD]
            kv_push(h, h, 0, upper, v_send, v_recv, v_own)

    pl.loop(0, early // 2)(v_pair)

    for n, p in enumerate(planes, 1):
        id_hop(n, p, p).wait_recv()
    idg[me] = functools.reduce(jnp.add, [idz[p] for p in range(seqs)])
    for d in peers:
        remote(idg.at[me], idg.at[me], i_send, i_recv, (d, z)).start()

    pl.loop(early // 2, KVH // 2)(v_pair)

    for n, w in enumerate(bits):
        kv_push(plain + n, KVH + n, w, upper, v_send, v_recv, v_own)

    def hop(up, t, origin, item, part=None):
        step = 1 if up else -1
        block = kvz.at[origin, item] if part is None else kvz.at[origin, item, :, part]
        return remote(
            block, block,
            z_send.at[(0 if up else 1) * seqs + t, item], z_recv.at[origin, item], (me, z + step),
        )

    def leave(item, part):
        @pl.when(z + 1 < seqs)
        def _():
            hop(True, 0, z, item, part).start()

        @pl.when(z > 0)
        def _():
            hop(False, 0, z, item, part).start()

    def v_leave(item):
        kv_all(item, upper, v_send, v_recv).wait_recv()
        kv_own(item, upper, v_own).wait()
        leave(item, upper)

    pl.loop(0, early)(v_leave)

    def ids_all():
        some = idg.at[pl.ds(0, dps - 1)]
        return remote(some, some, i_send, i_recv, (me, z))

    ids_all().wait_recv()
    ids = jnp.concatenate([idg[d, 0:1, :] for d in range(dps)], axis=0)
    first = jnp.full((dps, LANES), float(group), f32)
    for u in range(seqs * upd):
        same = ids == ids[:, u : u + 1]
        first = jnp.where(same, jnp.minimum(first, float(u * UNIT)), first)
    firsts[...] = first

    def starts(spots, table):
        unit = jnp.floor(spots * (1.0 / UNIT))
        hit = lane.astype(f32) == unit
        return jnp.sum(jnp.where(hit, table, 0.0), axis=1, keepdims=True)

    freqs = jnp.zeros((1, HD), f32)
    for j, freq in enumerate(frequencies()):
        freqs = jnp.where(lane % (HD // 2) == j, freq, freqs)
    table = jnp.concatenate(
        [jnp.broadcast_to(first[d : d + 1], (slab, LANES)) for d in range(dps)], axis=0
    )
    angles = (spot_up - starts(spot_up, table)) * freqs
    cosine = jnp.cos(angles)
    sine = jnp.sin(angles) * jnp.where(lane < HD // 2, -1.0, 1.0)

    k_load.wait()

    @pl.loop(0, KVH // 2)
    def _(pair):
        both = dot(onehot[...], kraw[:, cols(pair, 2 * HD)])
        for n in range(2):
            h = pair * 2 + n
            kvs[h, :, :HD] = turn(both[:, n * HD : (n + 1) * HD], cosine, sine)
            kv_push(h, h, 0, lower, k_send, k_recv, k_own)

    for n, w in enumerate(bits):
        kv_push(plain + n, KVH + n, w, lower, k_send, k_recv, k_own)

    def spots_all():
        some = sgot.at[pl.ds(0, dps - 1)]
        return remote(some, some, s_send, s_recv, (me, z))

    spots_all().wait_recv()
    strips = []
    for start in range(0, rows, LANES):
        strip = jnp.zeros((8, LANES), f32)
        for d in range(start // slab, (start + LANES) // slab):
            off = d * slab - start
            inside = (lane >= off) & (lane < off + slab)
            strip = jnp.where(inside, pltpu.roll(sgot[d], off, 1) if off else sgot[d], strip)
        strips.append(strip)
    zspots[z] = jnp.concatenate(strips, axis=1)

    def spots_hop(n, p, origin):
        block = zspots.at[origin]
        return remote(block, block, zs_send.at[n - 1], zs_recv.at[origin], (me, p))

    for n, p in enumerate(planes, 1):
        spots_hop(n, p, z).start()

    pl.loop(early, items)(v_leave)

    def q_turn(h):
        q_in(h).wait()
        x = dot(onehot[...], qs[h])
        for g in range(per_kv):
            qs[h, :, g * HD : (g + 1) * HD] = turn(x[:, g * HD : (g + 1) * HD], cosine, sine)

    def q_plain(h):
        q_turn(h)
        for d in peers:
            remote(
                qs.at[h, slab_of(d)], qr.at[h, slab_of(me)],
                q_send.at[h], q_recv.at[h], (d, z),
            ).start()
        pltpu.make_async_copy(
            qs.at[h, slab_of(me)], qr.at[h, slab_of(me)], q_own.at[h]
        ).start()

    def spot_in(sel, rank):
        return pl.ds(pl.multiple_of(sel * hr + rank * slab, slab), slab)

    def q_shared(h, w):
        q_turn(h)
        for sel in range(2):
            for d in side(w):
                remote(
                    qs.at[h, slab_of(flip(d, w) if sel else d)], qr.at[h, spot_in(sel, rank_of(me, w))],
                    q_send.at[h], q_recv.at[h], (d, z),
                ).start()
            pltpu.make_async_copy(
                qs.at[h, slab_of(flip(me, w) if sel else me)], qr.at[h, spot_in(sel, rank_of(me, w))],
                q_own.at[h],
            ).start()

    def o_plain(h):
        for d in peers:
            remote(
                ob.at[h, slab_of(d)], home.at[h, slab_of(me)],
                o_send.at[h], o_recv.at[h], (d, z),
            ).start()
        pltpu.make_async_copy(
            ob.at[h, slab_of(me)], home.at[h, slab_of(me)], o_own.at[h]
        ).start()

    def o_shared(h, item, w, sel):
        target = slab_of(flip(me, w) if sel else me)
        for d in side(w):
            remote(
                ob.at[h, spot_in(sel, rank_of(d, w))], home.at[h, target],
                o_send.at[item], o_recv.at[item], (d, z),
            ).start()
        pltpu.make_async_copy(
            ob.at[h, spot_in(sel, rank_of(me, w))], home.at[h, target], o_own.at[item]
        ).start()

    def away(buf, h, index, send, recv, count):
        block = buf.at[h, pl.ds(0, count)]
        return remote(block, block, send.at[index], recv.at[index], (me, z))

    def stay(buf, h, index, own, count):
        block = buf.at[h, pl.ds(0, count)]
        return pltpu.make_async_copy(block, block, own.at[index])

    def arrival(s):
        inner = s % chunk
        return (inner // share) * (seqs * share) + (s // chunk) * share + inner % share

    def arrival_half(s):
        inner = s % (chunk // 2)
        return (inner // share) * slab + (s // (chunk // 2)) * share + inner % share

    def source_half(s, w):
        inner = s % (chunk // 2)
        rank = inner // share
        d = (rank // w) * (2 * w) + ((me // w) % 2) * w + rank % w
        return d * slab + (s // (chunk // 2)) * share + inner % share

    def orders():
        sort[...] = jnp.where(col == arrival(row), 1.0, 0.0).astype(bf16)
        unsort[...] = jnp.where(row == arrival(col), 1.0, 0.0).astype(bf16)
        row_half, col_half = row[:hr, :hr], col[:hr, :hr]
        sort_half[...] = jnp.where(col_half == arrival_half(row_half), 1.0, 0.0).astype(bf16)
        unsort_half[...] = jnp.where(row_half == arrival_half(col_half), 1.0, 0.0).astype(bf16)

    def halves(x):
        top = jnp.floor(x * (1.0 / 32.0))
        return jnp.concatenate([top, x - 32.0 * top], axis=0).astype(bf16)

    def prepare():
        for n, p in enumerate(planes, 1):
            spots_hop(n, p, p).wait_recv()
        planed = []
        for p in range(seqs):
            s = dot_t(halves(zspots[p]), sort[...])
            planed.append(s[0:8] * 32.0 + s[8:16])
        keyed = []
        for start in range(0, group, LANES):
            strip = jnp.zeros((8, LANES), f32)
            for piece in range(start // chunk, (start + LANES) // chunk):
                c, p = piece // seqs, piece % seqs
                source = c * chunk
                base = source // LANES * LANES
                off = piece * chunk - start
                moved = planed[p][:, base : base + LANES]
                shift = (off - (source - base)) % LANES
                if shift:
                    moved = pltpu.roll(moved, shift, 1)
                strip = jnp.where((lane >= off) & (lane < off + chunk), moved, strip)
            keyed.append(strip)
        key = jnp.concatenate(keyed, axis=1)

        def fence(order, low_row, count, spots, key_row, owner):
            begin = starts(spots, firsts[pl.ds(owner, 1), :])
            keep = (key[key_row : key_row + 1] <= spots) & (key[key_row : key_row + 1] >= begin)
            bias[order, low_row : low_row + count] = jnp.where(keep, 0.0, -1e30)

        here = halves(zspots[z])
        up = dot_t(sort[...], here)
        fence(0, 0, rows, up[:, 0:1] * 32.0 + up[:, 8:9], 0, me)
        for n, w in enumerate(bits):
            pick = jnp.where(col[:hr] == source_half(row[:hr], w), 1.0, 0.0).astype(bf16)
            up = dot_t(pick, here)
            fence(n + 1, 0, hr, up[:, 0:1] * 32.0 + up[:, 8:9], 0, me)
            m = n + 1
            spots = up[:, m : m + 1] * 32.0 + up[:, m + 8 : m + 9]
            fence(n + 1, hr, hr, spots, m, flip(me, w))

    def attend(h, item, order, base, count, forth, back):
        here = pl.ds(base, count)
        x = dot(forth[...], qr[h, here]).astype(bf16)
        piece = count // seqs
        for p in range(seqs):
            both = dot(sort[...], kvz[p, item]).astype(bf16)
            for c in range(seqs):
                spot_rows = slice(c * rows + p * chunk, c * rows + (p + 1) * chunk)
                ks[spot_rows] = both[c * chunk : (c + 1) * chunk, :HD]
                vs[spot_rows] = both[c * chunk : (c + 1) * chunk, HD:]
        for c in range(seqs):
            reach = (c + 1) * rows
            inner = slice(c * piece, (c + 1) * piece)
            block = jnp.concatenate(
                [x[inner, g * HD : (g + 1) * HD] for g in range(per_kv)], axis=0
            )
            s = dot_t(block, ks[:reach])
            s = s.reshape(per_kv, piece, reach) * (HD ** -0.5 * LOG2E)
            s = s + bias[order, pl.ds(base + c * piece, piece), :reach][None]
            e = jnp.exp2(s - jnp.max(s, axis=-1, keepdims=True))
            total = jnp.sum(e, axis=-1, keepdims=True).reshape(per_kv * piece, 1)
            mixed = dot(e.astype(bf16).reshape(per_kv * piece, reach), vs[:reach])
            mixed = (mixed / total).astype(bf16)
            for g in range(per_kv):
                part_q[inner, g * HD : (g + 1) * HD] = mixed[g * piece : (g + 1) * piece]
        ob[h, here] = dot(back[...], part_q[:count]).astype(bf16)

    def finish(h):
        away(home, h, h, o_send, o_recv, rows - slab).wait_recv()
        stay(home, h, h, o_own, slab).wait()
        out[:, cols(h, wide)] = dot(onehot_t[...], home[h]).astype(bf16)

    def finish_shared(h, n):
        for item in (h, KVH + n):
            away(home, h, item, o_send, o_recv, hr - slab).wait_recv()
            stay(home, h, item, o_own, slab).wait()
        out[:, cols(h, wide)] = dot(onehot_t[...], home[h]).astype(bf16)

    @pl.loop(0, items + seqs - 1)
    def _(i):
        @pl.when(i < items)
        def _():
            kv_all(i, lower, k_send, k_recv).wait_recv()
            kv_own(i, lower, k_own).wait()
            leave(i, lower)

        for t in range(1, seqs):
            live = (i >= t) & (i - t < items)

            @pl.when(live & (z >= t))
            def _():
                hop(True, t, z - t, i - t).wait_recv()

                @pl.when(z + 1 < seqs)
                def _():
                    hop(True, t, z - t, i - t).start()

            @pl.when(live & (z + t < seqs))
            def _():
                hop(False, t, z + t, i - t).wait_recv()

                @pl.when(z > 0)
                def _():
                    hop(False, t, z + t, i - t).start()

        @pl.when(i < plain // 2)
        def _():
            q_plain(2 * i)
            q_plain(2 * i + 1)

        @pl.when(i == plain // 2)
        def _():
            for h in range(plain // 2 * 2, plain):
                q_plain(h)
            for n, w in enumerate(bits):
                q_shared(plain + n, w)

        @pl.when(i == min(2, seqs - 1))
        def _():
            orders()
            prepare()

        j = i - (seqs - 1)

        @pl.when((j >= 0) & (j < plain))
        def _():
            away(qr, j, j, q_send, q_recv, rows - slab).wait_recv()
            stay(qr, j, j, q_own, slab).wait()
            attend(j, j, 0, 0, rows, sort, unsort)
            o_plain(j)

        if nsh:
            @pl.when((j >= plain) & (j < KVH))
            def _():
                away(qr, j, j, q_send, q_recv, rows - 2 * slab).wait_recv()
                stay(qr, j, j, q_own, 2 * slab).wait()

            @pl.when(j >= plain)
            def _():
                n = (j - plain) % nsh
                sel = (j - plain) // nsh
                base = pl.multiple_of(sel * hr, hr)
                attend(plain + n, j, n + 1, base, hr, sort_half, unsort_half)

            for sel in range(2):
                for n, w in enumerate(bits):
                    @pl.when(j == plain + sel * nsh + n)
                    def _():
                        o_shared(plain + n, plain + sel * nsh + n, w, sel)


    pl.loop(0, plain)(finish)
    for n in range(nsh):
        finish_shared(plain + n, n)

    ids_all().wait_send()
    spots_all().wait_send()
    for n, p in enumerate(planes, 1):
        id_hop(n, p, z).wait_send()
        spots_hop(n, p, z).wait_send()

    @pl.loop(0, items)
    def _(item):
        kv_all(item, upper, v_send, v_recv).wait_send()
        kv_all(item, lower, k_send, k_recv).wait_send()
        for t in range(seqs - 1):

            @pl.when((z >= t) & (z + 1 < seqs))
            def _():
                hop(True, t, z - t, item).wait_send()

            @pl.when((z + t < seqs) & (z > 0))
            def _():
                hop(False, t, z + t, item).wait_send()

    @pl.loop(0, plain)
    def _(h):
        away(qr, h, h, q_send, q_recv, rows - slab).wait_send()
        away(ob, h, h, o_send, o_recv, rows - slab).wait_send()

    for n in range(nsh):
        h = plain + n
        away(qr, h, h, q_send, q_recv, rows - 2 * slab).wait_send()
        for item in (h, KVH + n):
            away(ob, h, item, o_send, o_recv, hr - slab).wait_send()


def per_device(queries, keys, values, plan, segment_ids):
    rows = queries.shape[0]
    seqs = lax.axis_size("seq")
    dps = lax.axis_size("dp")
    group = rows * seqs
    per_kv = H // KVH
    wide = per_kv * HD
    nsh = len(shared_bits(dps))
    items = KVH + nsh
    anywhere = pl.BlockSpec(memory_space=pltpu.HBM)
    dma = pltpu.SemaphoreType.DMA
    bf16, f32, i32 = jnp.bfloat16, jnp.float32, jnp.int32
    return pl.pallas_call(
        functools.partial(travel, seqs, dps),
        in_specs=[anywhere] * 5,
        out_specs=pl.BlockSpec(memory_space=pltpu.VMEM),
        out_shape=pltpu.VMEM(queries.shape, bf16),
        scratch_shapes=[
            pltpu.VMEM((1, rows), i32),
            pltpu.VMEM((1, rows), i32),
            pltpu.VMEM((rows, KVH * HD), bf16),
            pltpu.VMEM((rows, KVH * HD), bf16),
            pltpu.VMEM((KVH, rows, wide), bf16),
            pltpu.VMEM((KVH, rows, 2 * HD), bf16),
            pltpu.VMEM((KVH, rows, wide), bf16),
            pltpu.VMEM((seqs, items, rows, 2 * HD), bf16),
            pltpu.VMEM((KVH, rows, wide), bf16),
            pltpu.VMEM((KVH, rows, wide), bf16),
            pltpu.VMEM((group, HD), bf16),
            pltpu.VMEM((group, HD), bf16),
            pltpu.VMEM((rows, rows), bf16),
            pltpu.VMEM((rows, rows), bf16),
            pltpu.VMEM((rows, rows), bf16),
            pltpu.VMEM((rows, rows), bf16),
            pltpu.VMEM((rows // 2, rows // 2), bf16),
            pltpu.VMEM((rows // 2, rows // 2), bf16),
            pltpu.VMEM((1 + nsh, rows, group), f32),
            pltpu.VMEM((dps, LANES), f32),
            pltpu.VMEM((rows, wide), bf16),
            pltpu.VMEM((dps, 8, LANES), f32),
            pltpu.VMEM((dps, 8, LANES), f32),
            pltpu.VMEM((seqs, 8, rows), f32),
            pltpu.VMEM((seqs, 8, LANES), f32),
            pltpu.VMEM((dps, 8, LANES), f32),
            dma((2,)), dma((2,)), dma((KVH,)),
            dma((items,)), dma((items,)), dma((items,)),
            dma((items,)), dma((items,)), dma((items,)),
            dma((KVH,)), dma((KVH,)), dma((KVH,)),
            dma((items,)), dma((items,)), dma((items,)),
            dma, dma, dma((seqs,)), dma((seqs,)), dma, dma, dma((seqs,)), dma((seqs,)),
            dma((2 * seqs, items)), dma((seqs, items)),
        ],
        compiler_params=pltpu.CompilerParams(
            collective_id=0, has_side_effects=True, vmem_limit_bytes=56 * 1024 * 1024
        ),
    )(queries, keys, values, plan[None, :], segment_ids[None, :])


def solution(mesh):
    return jax.shard_map(
        per_device,
        mesh=mesh,
        in_specs=(
            P(("dp", "seq"), None),
            P(("dp", "seq"), None),
            P(("dp", "seq"), None),
            P(("dp", "seq")),
            P(("dp", "seq")),
        ),
        out_specs=P(("dp", "seq"), None),
        check_vma=False,
    )
```
